512 devices in a mesh: section: 16 (over y, z_lo), expert: 32 (over z_hi, x, core).
Axes of the slice: x: 4, y: 8, z: 8 (z_hi: 4, z_lo: 2; z = z_hi * 2 + z_lo), core: 2. Of those that a mesh axis runs over, the one named last changes fastest.
Arguments:
- pre_gate_a: bfloat16 [16, 512, 4096], P('section', None, 'expert'), may hold values from -6 to 6
- pre_gate_b: bfloat16 [16, 512, 4096], P('section', None, 'expert'), may hold values from -6 to 6
- pre_up_a: bfloat16 [16, 512, 4096], P('section', None, 'expert'), may hold values from -6 to 6
- pre_up_b: bfloat16 [16, 512, 4096], P('section', None, 'expert'), may hold values from -6 to 6
- grads_a: bfloat16 [16, 2048, 3584], P('section', 'expert'), may hold values from -2 to 2
- grads_b: bfloat16 [16, 2048, 3584], P('section', 'expert'), may hold values from -2 to 2
- route_a: int32 [16, 2048, 1], P('section', 'expert'), may hold values from 0 to 3; in each aligned block of 64 rows (0 to 63, 64 to 127, ..., all dimensions but the last counted through in order) at most 16 rows name the same one
- route_b: int32 [16, 2048, 1], P('section', 'expert'), may hold values from 0 to 3; in each aligned block of 64 rows (0 to 63, 64 to 127, ..., all dimensions but the last counted through in order) at most 16 rows name the same one
- probs_a: float32 [16, 2048, 1], P('section', 'expert'), may hold values from 0.1 to 1
- probs_b: float32 [16, 2048, 1], P('section', 'expert'), may hold values from 0.1 to 1
- w_gate: bfloat16 [16, 3584, 4096], P('section', None, 'expert'), may hold values from -0.09375 to 0.09375
- w_up: bfloat16 [16, 3584, 4096], P('section', None, 'expert'), may hold values from -0.09375 to 0.09375
- w_down: bfloat16 [16, 4096, 3584], P('section', 'expert'), may hold values from -0.1875 to 0.1875
Outputs:
- dx_a: bfloat16 [16, 2048, 3584], P('section', 'expert')
- dx_b: bfloat16 [16, 2048, 3584], P('section', 'expert')
- dprob_a: float32 [16, 2048, 1], P('section', 'expert')
- dprob_b: float32 [16, 2048, 1], P('section', 'expert')
The draws below stay inside these ranges and needn't reach their ends.
Inputs may be any that keep to these rules, and one draw needn't show every extreme that they name: `route_a`: each token names one expert; among the 64 tokens of one device's block every expert is named exactly 16 times. `route_b`: as for route_a.
All inputs are finite; a program needn't handle non-finite values.
Results may differ from the reference program's by a relative error of at most 0.0085.
Values may be sent and summed in bfloat16 or wider, within the bound.
No kernel may reach another device: no remote copies, remote signals or barrier semaphores. Data moves between devices by JAX's collectives and lax.ppermute only.
A program may use at most 64 MiB of HBM per device.

```python
import math
import jax
import jax.numpy as jnp
import numpy as np
from jax import lax

D = 3584
H = 1024
EXPERTS = 4
TOP = 1
TOK = 64
CAP = 16
TOKENS = 2048
N_SECTION = 16
N_EXPERT = 32


def shard_levels(rng, shape, pieces, least, high):
    def one(dim, blocks):
        heights = jax.random.uniform(jax.random.fold_in(jax.random.fold_in(rng, 6), dim), (blocks,), jnp.float32, least / len(pieces), high / len(pieces))
        return jnp.repeat(jnp.exp(heights), shape[dim] // blocks).reshape((-1,) + (1,) * (len(shape) - dim - 1))

    loudness = one(*pieces[0])
    for cut in pieces[1:]:
        loudness = loudness * one(*cut)
    return loudness


def assign_block(key, own, number, rows, amount, top, limit, lean):
    order = jax.random.permutation(key, amount)
    crowded, ordinary = load_shares(amount, rows * top, limit, lean, True), load_shares(amount, rows * top, limit, lean, False)
    places = jnp.arange(amount)

    def named(sizes, offset_by):
        used = int((sizes > 0).sum())
        fixed = max(1, used // 4)
        shifted = fixed + (places - fixed + offset_by * (used - fixed)) % max(1, amount - fixed)
        return jnp.zeros((amount,), jnp.int32).at[order[jnp.where(places < fixed, places, shifted)]].set(jnp.asarray(sizes, jnp.int32))

    sizes = jnp.where(number % 4 == 0, named(crowded, number // 4), named(ordinary, number - number // 4 - 1))
    mixed = jax.random.permutation(jax.random.fold_in(own, 3), amount)
    source_of, receiver = mixed[0:amount // 2 * 2:2], mixed[1:amount // 2 * 2:2]
    margin = jnp.minimum(sizes[source_of] - 1, limit - sizes[receiver]) // 2
    margin = jnp.where((source_of == order[0]) | (receiver == order[0]) | (sizes[receiver] == 0), 0, jnp.maximum(margin, 0))
    shifted = jax.random.randint(jax.random.fold_in(own, 4), (amount // 2,), 0, 1 << 20) % (margin + 1)
    sizes = sizes.at[source_of].add(-shifted).at[receiver].add(shifted)
    members = jnp.searchsorted(jnp.cumsum(sizes), jnp.arange(rows * top), side="right").astype(jnp.int32)
    listing = members.reshape(top, rows).T
    listing = listing[jax.random.permutation(jax.random.fold_in(own, 1), rows)]
    offset_by = jax.random.randint(jax.random.fold_in(own, 2), (rows, 1), 0, top)
    return jnp.take_along_axis(listing, (jnp.arange(top)[None, :] + offset_by) % top, axis=1)


def load_shares(number_of, total, reach, lean, full):
    portions = [(1 << 20) // math.isqrt(grade ** lean) + 1 for grade in range(1, number_of + 1)]
    largest = reach if full else min(reach, max(-(-total // number_of), total * portions[0] // sum(portions)))
    least = 1 if total - largest >= number_of - 1 else 0
    counts, surplus = [largest] + [least] * (number_of - 1), total - largest - least * (number_of - 1)
    while surplus > 0:
        movable = [i for i in range(1, number_of) if counts[i] < largest] or [i for i in range(1, number_of) if counts[i] < reach]
        pool, left = sum([portions[i] for i in movable]), surplus
        for i in movable:
            addition = min(reach - counts[i], max(1, left * portions[i] // pool), surplus)
            counts[i] = counts[i] + addition
            surplus = surplus - addition
    return np.array(counts)


def scatter_about(own_key, shape, scale, limit, pieces=(), kind=jnp.bfloat16):
    gain = shard_levels(own_key, shape, pieces, -0.22, 0.18) if pieces else 1.0
    array = jax.random.normal(own_key, shape, jnp.float32) * scale * gain
    return jnp.minimum(jnp.maximum(array, -limit), limit).astype(kind)


def setup_inputs(seed: int = 0) -> dict:
    arg_keys = jax.random.split(jax.random.key(seed), 14)
    pre_gate_a = scatter_about(arg_keys[0], (N_SECTION, N_EXPERT * CAP, EXPERTS * H), 1.0, 6.0, ((0, 16), (2, 32)))
    pre_gate_b = scatter_about(arg_keys[1], (N_SECTION, N_EXPERT * CAP, EXPERTS * H), 1.0, 6.0, ((0, 16), (2, 32)))
    pre_up_a = scatter_about(arg_keys[2], (N_SECTION, N_EXPERT * CAP, EXPERTS * H), 1.0, 6.0, ((0, 16), (2, 32)))
    pre_up_b = scatter_about(arg_keys[3], (N_SECTION, N_EXPERT * CAP, EXPERTS * H), 1.0, 6.0, ((0, 16), (2, 32)))
    grads_a = scatter_about(arg_keys[4], (N_SECTION, TOKENS, D), 0.3, 2.0, ((0, 16), (1, 32)))
    grads_b = scatter_about(arg_keys[5], (N_SECTION, TOKENS, D), 0.3, 2.0, ((0, 16), (1, 32)))
    route_a_keys = jax.random.split(jax.random.fold_in(arg_keys[6], 1), N_SECTION * TOKENS // TOK)
    route_a_turns = jax.random.permutation(jax.random.fold_in(arg_keys[6], 3), N_SECTION * TOKENS // TOK)
    route_a = jax.vmap(lambda own, number: assign_block(jax.random.fold_in(arg_keys[6], 2), own, number, TOK, EXPERTS, TOP, CAP, 1))(route_a_keys, route_a_turns).reshape((N_SECTION, TOKENS, TOP))
    route_b_keys = jax.random.split(jax.random.fold_in(arg_keys[7], 1), N_SECTION * TOKENS // TOK)
    route_b_turns = jax.random.permutation(jax.random.fold_in(arg_keys[7], 3), N_SECTION * TOKENS // TOK)
    route_b = jax.vmap(lambda own, number: assign_block(jax.random.fold_in(arg_keys[7], 2), own, number, TOK, EXPERTS, TOP, CAP, 1))(route_b_keys, route_b_turns).reshape((N_SECTION, TOKENS, TOP))
    probs_a = jnp.clip(0.1 + 0.9 * jax.random.uniform(arg_keys[8], (N_SECTION, TOKENS, TOP), jnp.float32) ** shard_levels(arg_keys[8], (N_SECTION, TOKENS, TOP), ((0, 16), (1, 32)), -0.2, 0.2), 0.1, 1.0)
    probs_b = jnp.clip(0.1 + 0.9 * jax.random.uniform(arg_keys[9], (N_SECTION, TOKENS, TOP), jnp.float32) ** shard_levels(arg_keys[9], (N_SECTION, TOKENS, TOP), ((0, 16), (1, 32)), -0.2, 0.2), 0.1, 1.0)
    w_gate = scatter_about(arg_keys[10], (N_SECTION, D, EXPERTS * H), D ** -0.5, 0.09375, ((0, 16), (2, 32)))
    w_up = scatter_about(arg_keys[11], (N_SECTION, D, EXPERTS * H), D ** -0.5, 0.09375, ((0, 16), (2, 32)))
    w_down = scatter_about(arg_keys[12], (N_SECTION, EXPERTS * H, D), H ** -0.5, 0.1875, ((0, 16), (1, 32)))
    return {"pre_gate_a": pre_gate_a, "pre_gate_b": pre_gate_b, "pre_up_a": pre_up_a, "pre_up_b": pre_up_b, "grads_a": grads_a, "grads_b": grads_b, "route_a": route_a, "route_b": route_b, "probs_a": probs_a, "probs_b": probs_b, "w_gate": w_gate, "w_up": w_up, "w_down": w_down}


def silu_parts(gate):
    sig = jax.nn.sigmoid(gate)
    return gate * sig, sig * (1.0 + gate * (1.0 - sig))


def slots_of(route):
    onehot = (route[..., None] == jnp.arange(EXPERTS, dtype=jnp.int32)).astype(jnp.int32)
    flat = onehot.reshape(N_EXPERT, TOK * TOP, EXPERTS)
    rank = jnp.cumsum(flat, axis=1) - flat
    return jnp.sum(rank * flat, axis=-1).reshape(TOKENS, TOP).astype(jnp.int32)


def one_batch(pre_gate, pre_up, upstream, route, probs, w_gate, w_up, w_down):
    group = N_EXPERT // EXPERTS
    width = H // group
    slot = slots_of(route)
    owner = jnp.broadcast_to((jnp.arange(TOKENS, dtype=jnp.int32) // TOK)[:, None], (TOKENS, TOP))
    token = jnp.broadcast_to(jnp.arange(TOKENS, dtype=jnp.int32)[:, None], (TOKENS, TOP))
    rows_d = jnp.zeros((EXPERTS, N_EXPERT, CAP, D), jnp.bfloat16).at[route, owner, slot].set(upstream[token])
    saved_g = jnp.transpose(pre_gate.reshape(N_EXPERT * CAP, EXPERTS, H), (1, 0, 2))
    saved_u = jnp.transpose(pre_up.reshape(N_EXPERT * CAP, EXPERTS, H), (1, 0, 2))
    gates = jnp.transpose(w_gate.reshape(D, EXPERTS, H), (1, 0, 2))
    ups = jnp.transpose(w_up.reshape(D, EXPERTS, H), (1, 0, 2))
    downs = w_down.reshape(EXPERTS, H, D)

    def expert(operands):
        block_d, pre_g, pre_u, g_w, u_w, d_w = operands
        flat_d = block_d.reshape(-1, D)
        gate = pre_g.astype(jnp.float32)
        up = pre_u.astype(jnp.float32)
        act, slope = silu_parts(gate)
        hidden = act * up
        grad_h = jnp.dot(flat_d, d_w.T, preferred_element_type=jnp.float32)
        share = jnp.sum((grad_h * hidden).reshape(-1, group, width), axis=-1)
        share = jnp.sum(share.astype(jnp.bfloat16).astype(jnp.float32), axis=-1)
        grad_g = (grad_h * up * slope).astype(jnp.bfloat16).astype(jnp.float32).reshape(-1, group, width)
        grad_u = (grad_h * act).astype(jnp.bfloat16).astype(jnp.float32).reshape(-1, group, width)
        gate_w = g_w.astype(jnp.float32).reshape(D, group, width)
        up_w = u_w.astype(jnp.float32).reshape(D, group, width)
        part = jnp.einsum('rgk,dgk->rgd', grad_g, gate_w) + jnp.einsum('rgk,dgk->rgd', grad_u, up_w)
        total = jnp.sum(part.astype(jnp.bfloat16).astype(jnp.float32), axis=1)
        return total.reshape(N_EXPERT, CAP, D), share.reshape(N_EXPERT, CAP)

    parts, shares = lax.map(expert, (rows_d, saved_g, saved_u, gates, ups, downs))
    picked = parts[route, owner, slot]
    grad_x = jnp.sum(probs[..., None] * picked, axis=1).astype(jnp.bfloat16)
    return grad_x, shares[route, owner, slot]


def reference(pre_gate_a, pre_gate_b, pre_up_a, pre_up_b, grads_a, grads_b, route_a, route_b, probs_a, probs_b, w_gate, w_up, w_down):
    upper = jnp.roll(grads_a, -1, axis=0)
    lower = jnp.roll(grads_b, 1, axis=0)

    def section_work(operands):
        ga, gb, pua, pub, ua, ub, ra, rb, pa, pb, g_w, u_w, d_w = operands
        dxa, dpa = one_batch(ga, pua, ua, ra, pa, g_w, u_w, d_w)
        dxb, dpb = one_batch(gb, pub, ub, rb, pb, g_w, u_w, d_w)
        return dxa, dxb, dpa, dpb

    dx_a, dx_b, dprob_a, dprob_b = lax.map(section_work, (pre_gate_a, pre_gate_b, pre_up_a, pre_up_b, upper, lower, route_a, route_b, probs_a, probs_b, w_gate, w_up, w_down))
    return (dx_a, dx_b, dprob_a, dprob_b)
```

```python
import jax
import jax.numpy as jnp
from jax import lax
from jax.experimental import pallas as pl
from jax.experimental.pallas import tpu as pltpu
from jax.sharding import PartitionSpec as P

EXPERTS = 4
CAP = 16
NX = 4
NC = 2
PAD = 128


def place(z, x, c):
    return (z % EXPERTS) * NX * NC + (x % NX) * NC + c


def ring(dx=0, dc=0):
    return [
        (place(z, x, c), place(z, x + dx, c ^ dc))
        for z in range(EXPERTS)
        for x in range(NX)
        for c in range(NC)
    ]


def columns():
    return [[place(z, x, c) for z in range(EXPERTS)] for x in range(NX) for c in range(NC)]


def to_x(value, dx):
    return lax.ppermute(value, "expert", ring(dx=dx))


def to_core(value):
    return lax.ppermute(value, "expert", ring(dc=1))


def over_z(value):
    return lax.all_to_all(
        value, "expert", split_axis=0, concat_axis=0, axis_index_groups=columns(), tiled=True
    )


def passed_along(value, steps):
    count = lax.axis_size("section")
    pairs = [(source, (source + steps) % count) for source in range(count)]
    return lax.ppermute(value, "section", pairs)


def slots_of(route):
    onehot = (route == jnp.arange(EXPERTS, dtype=jnp.int32)[None, :]).astype(jnp.float32)
    size = onehot.shape[0]
    before = jnp.tril(jnp.ones((size, size), jnp.float32), -1)
    rank = jnp.dot(before, onehot)
    slot = jnp.sum(rank * onehot, axis=-1, keepdims=True).astype(jnp.int32)
    return route * CAP + slot


def table(place_of):
    lanes = jnp.arange(EXPERTS * CAP, dtype=jnp.int32)[None, :]
    return (place_of == lanes).astype(jnp.bfloat16)


def nt(a, b):
    return lax.dot_general(a, b, (((1,), (1,)), ((), ())), preferred_element_type=jnp.float32)


def expert_kernel(
    pos, own, left, right, opp0, opp1,
    gate_own, up_own, gate_sib, up_sib,
    wd_own, wd_sib, wg_own, wg_sib, wu_own, wu_sib,
    p_own, p_left, p_right, p_opp,
):
    x = pos[0]
    c = pos[1]
    wide = own.shape[-1]
    rows = jnp.concatenate(
        [opp0[...], opp1[...], own[...], right[...], left[...]], axis=0
    )
    wd = jnp.concatenate([wd_own[...], wd_sib[...]], axis=0)
    dh = nt(rows, wd)
    shifts = (2, 0, 1, 3)

    def saved(mine, other):
        blocks = []
        for k in shifts:
            xs = (x + k) % NX
            for z in range(EXPERTS):
                blocks.append(
                    jnp.concatenate(
                        [mine[z * NX * NC + xs * NC + c], other[z * NX + xs]], axis=-1
                    )
                )
        return jnp.concatenate(blocks, axis=0).astype(jnp.float32)

    gate = saved(gate_own, gate_sib)
    up = saved(up_own, up_sib)
    sig = jax.nn.sigmoid(gate)
    act = gate * sig
    slope = sig * (1.0 + gate * (1.0 - sig))
    q = jnp.sum(dh * (act * up), axis=-1, keepdims=True)
    dg = (dh * up * slope).astype(jnp.bfloat16)
    du = (dh * act).astype(jnp.bfloat16)
    both = jnp.concatenate([dg, du], axis=-1)
    weights = jnp.concatenate([wg_own[...], wg_sib[...], wu_own[...], wu_sib[...]], axis=-1)
    part = nt(both, weights).astype(jnp.bfloat16)
    q = jnp.broadcast_to(q, (q.shape[0], PAD)).astype(jnp.bfloat16)
    n = own.shape[0]
    for k, out in enumerate((p_opp, p_own, p_right, p_left)):
        out[:, :wide] = part[k * n:(k + 1) * n]
        out[:, wide:] = q[k * n:(k + 1) * n]


def expert_work(pos, pieces, saved, weights):
    own = pieces[0]
    count, wide = own.shape
    shape = jax.ShapeDtypeStruct((count, wide + PAD), jnp.bfloat16)
    vmem = pl.BlockSpec(memory_space=pltpu.VMEM)
    return pl.pallas_call(
        expert_kernel,
        in_specs=[pl.BlockSpec(memory_space=pltpu.SMEM)] + [vmem] * 15,
        out_specs=[vmem] * 4,
        out_shape=[shape] * 4,
        name="expert_work",
    )(pos, *pieces, *saved, *weights)


def gather_x(own):
    half = own.shape[0] // 2
    left = to_x(own, 1)
    right = to_x(own, -1)
    opp0 = to_x(right[:half], -1)
    opp1 = to_x(left[half:], 1)
    return own, left, right, opp0, opp1


def add(a, b):
    return (a.astype(jnp.float32) + b.astype(jnp.float32)).astype(jnp.bfloat16)


def reduce_x(p_own, p_left, p_right, p_opp):
    half = p_own.shape[0] // 2
    from_left = to_x(p_opp[:half], 1)
    from_right = to_x(p_opp[half:], -1)
    p_right = jnp.concatenate([add(p_right[:half], from_left), p_right[half:]], axis=0)
    p_left = jnp.concatenate([p_left[:half], add(p_left[half:], from_right)], axis=0)
    from_left = to_x(p_right, 1)
    from_right = to_x(p_left, -1)
    total = p_own.astype(jnp.float32) + from_left.astype(jnp.float32)
    return (total + from_right.astype(jnp.float32)).astype(jnp.bfloat16)


def on_device(
    pre_gate_a, pre_gate_b, pre_up_a, pre_up_b, grads_a, grads_b,
    route_a, route_b, probs_a, probs_b, w_gate, w_up, w_down,
):
    upper = passed_along(grads_a[0], -1)
    lower = passed_along(grads_b[0], 1)
    me = lax.axis_index("expert")
    core = me % NC
    pos = jnp.stack([(me // NC) % NX, core]).astype(jnp.int32)
    pre = [v[0].reshape(-1, CAP, v.shape[-1]) for v in (pre_gate_a, pre_up_a, pre_gate_b, pre_up_b)]
    other = jnp.stack(
        [
            jnp.where(core == 0, v.reshape(-1, NC, CAP, v.shape[-1])[:, 1], v.reshape(-1, NC, CAP, v.shape[-1])[:, 0])
            for v in pre
        ]
    )
    other = to_core(other)
    wd, wg, wu = w_down[0], w_gate[0], w_up[0]
    weights = (wd, to_core(wd), wg, to_core(wg), wu, to_core(wu))

    def handle(arrived, route, probs, saved):
        place_of = slots_of(route)
        chosen = table(place_of)
        send = lax.dot_general(
            chosen, arrived, (((0,), (0,)), ((), ())), preferred_element_type=jnp.float32
        ).astype(jnp.bfloat16)
        wide = send.shape[-1]
        own = over_z(send.reshape(EXPERTS, CAP, wide)).reshape(EXPERTS * CAP, wide)
        parts = expert_work(pos, gather_x(own), saved, weights)
        total = reduce_x(*parts)
        back = over_z(total.reshape(EXPERTS, CAP, -1)).reshape(EXPERTS * CAP, -1)
        picked = jnp.dot(chosen, back, preferred_element_type=jnp.float32)
        grad_x = (probs * picked[:, :wide]).astype(jnp.bfloat16)
        return grad_x[None], picked[None, :, wide:wide + 1]

    dx_a, dprob_a = handle(upper, route_a[0], probs_a[0], (pre[0], pre[1], other[0], other[1]))
    dx_b, dprob_b = handle(lower, route_b[0], probs_b[0], (pre[2], pre[3], other[2], other[3]))
    return (dx_a, dx_b, dprob_a, dprob_b)


def solution(mesh):
    hidden = P("section", None, "expert")
    tokens = P("section", "expert", None)
    return jax.shard_map(
        on_device,
        mesh=mesh,
        in_specs=(hidden,) * 4 + (tokens,) * 6 + (hidden, hidden, tokens),
        out_specs=(tokens,) * 4,
        check_vma=False,
    )
```

```python
import jax
import jax.numpy as jnp
from jax import lax
from jax.experimental import pallas as pl
from jax.experimental.pallas import tpu as pltpu
from jax.sharding import PartitionSpec as P

EXPERTS = 4
CAP = 16
NX = 4
NC = 2
PAD = 128
TILE = 512


def place(z, x, c):
    return z * NX * NC + x * NC + c


def weight_partner(x, c):
    return (((x + c) ^ 1) + NX - c) % NX


def token_partner(x, c):
    return weight_partner(x, 1 - c)


def moved(value, rule):
    pairs = []
    for z in range(EXPERTS):
        for x in range(NX):
            for c in range(NC):
                to_x, to_c = rule(x, c)
                pairs.append((place(z, x, c), place(z, to_x, to_c)))
    return lax.ppermute(value, "expert", pairs)


def to_weight_partner(value):
    return moved(value, lambda x, c: (weight_partner(x, c), c))


def to_sibling(value):
    return moved(value, lambda x, c: (x, 1 - c))


def over_z(value):
    columns = [[place(z, x, c) for z in range(EXPERTS)] for x in range(NX) for c in range(NC)]
    return lax.all_to_all(
        value, "expert", split_axis=0, concat_axis=0, axis_index_groups=columns, tiled=True
    )


def passed_along(value, steps):
    count = lax.axis_size("section")
    pairs = [(source, (source + steps) % count) for source in range(count)]
    return lax.ppermute(value, "section", pairs)


def slots_of(route):
    onehot = (route == jnp.arange(EXPERTS, dtype=jnp.int32)[None, :]).astype(jnp.float32)
    size = onehot.shape[0]
    before = jnp.tril(jnp.ones((size, size), jnp.float32), -1)
    rank = jnp.dot(before, onehot)
    slot = jnp.sum(rank * onehot, axis=-1, keepdims=True).astype(jnp.int32)
    return route * CAP + slot


def table(place_of):
    lanes = jnp.arange(EXPERTS * CAP, dtype=jnp.int32)[None, :]
    return (place_of == lanes).astype(jnp.bfloat16)


def nt(a, b):
    return lax.dot_general(a, b, (((1,), (1,)), ((), ())), preferred_element_type=jnp.float32)


def expert_kernel(
    pos, own, sib, same, cross,
    gate_own, up_own, gate_mate, up_mate,
    wd_own, wd_mate, wg_own, wg_mate, wu_own, wu_mate,
    p_own, p_sib, p_same, p_cross,
    v_rows, v_gate_own, v_up_own, v_gate_mate, v_up_mate, v_wd, v_w, v_out, s_in, s_w, s_out,
):
    x, c, tp = pos[0], pos[1], pos[2]
    n, wide = own.shape
    unit = wd_own.shape[0]
    loads = []
    for k, ref in enumerate((own, sib, same, cross)):
        loads.append((ref, v_rows.at[pl.ds(k * n, n)]))
    loads.append((wd_own, v_wd.at[pl.ds(0, unit)]))
    loads.append((wd_mate, v_wd.at[pl.ds(unit, unit)]))
    loads += [(gate_own, v_gate_own), (up_own, v_up_own), (gate_mate, v_gate_mate), (up_mate, v_up_mate)]
    first = [pltpu.make_async_copy(a, b, s_in.at[k]) for k, (a, b) in enumerate(loads)]
    later = [
        pltpu.make_async_copy(ref, v_w.at[k], s_w.at[k])
        for k, ref in enumerate((wg_own, wg_mate, wu_own, wu_mate))
    ]
    for copy in first + later:
        copy.start()
    for copy in first:
        copy.wait()
    dh = None
    for d in range(0, wide, TILE):
        cut = slice(d, d + TILE)
        term = nt(v_rows[:, cut], v_wd[:, cut])
        dh = term if dh is None else dh + term

    def saved(mine, mate):
        blocks = []
        for slot, xs in ((0, x), (1, tp)):
            for cs in (c, 1 - c):
                for z in range(EXPERTS):
                    blocks.append(
                        jnp.concatenate(
                            [
                                mine[z * NX * NC + xs * NC + cs],
                                mate[(slot * EXPERTS + z) * NC + cs],
                            ],
                            axis=-1,
                        )
                    )
        return jnp.concatenate(blocks, axis=0).astype(jnp.float32)

    gate = saved(v_gate_own, v_gate_mate)
    up = saved(v_up_own, v_up_mate)
    sig = jax.nn.sigmoid(gate)
    act = gate * sig
    slope = sig * (1.0 + gate * (1.0 - sig))
    q = jnp.sum(dh * (act * up), axis=-1, keepdims=True)
    dg = (dh * up * slope).astype(jnp.bfloat16)
    du = (dh * act).astype(jnp.bfloat16)
    both = jnp.concatenate([dg, du], axis=-1)
    v_out[:, wide:] = jnp.broadcast_to(q, (q.shape[0], PAD)).astype(jnp.bfloat16)
    for copy in later:
        copy.wait()
    for d in range(0, wide, TILE):
        cut = slice(d, d + TILE)
        w = jnp.concatenate([v_w[k, cut] for k in range(4)], axis=-1)
        v_out[:, cut] = nt(both, w).astype(jnp.bfloat16)
    stores = [
        pltpu.make_async_copy(v_out.at[pl.ds(k * n, n)], out, s_out.at[k])
        for k, out in enumerate((p_own, p_sib, p_same, p_cross))
    ]
    for copy in stores:
        copy.start()
    for copy in stores:
        copy.wait()


def expert_work(pos, pieces, saved, weights):
    count, wide = pieces[0].shape
    unit = weights[0].shape[0]
    shape = jax.ShapeDtypeStruct((count, wide + PAD), jnp.bfloat16)
    anywhere = pl.BlockSpec(memory_space=pl.ANY)
    bf16 = jnp.bfloat16
    return pl.pallas_call(
        expert_kernel,
        in_specs=[pl.BlockSpec(memory_space=pltpu.SMEM)] + [anywhere] * 14,
        out_specs=[anywhere] * 4,
        out_shape=[shape] * 4,
        scratch_shapes=[
            pltpu.VMEM((4 * count, wide), bf16),
            *[pltpu.VMEM(v.shape, bf16) for v in saved],
            pltpu.VMEM((2 * unit, wide), bf16),
            pltpu.VMEM((4, wide, unit), bf16),
            pltpu.VMEM((4 * count, wide + PAD), bf16),
            pltpu.SemaphoreType.DMA((10,)),
            pltpu.SemaphoreType.DMA((4,)),
            pltpu.SemaphoreType.DMA((4,)),
        ],
        compiler_params=pltpu.CompilerParams(vmem_limit_bytes=32 << 20),
        name="expert_work",
    )(pos, *pieces, *saved, *weights)


def gather_rows(own):
    same = moved(own, lambda x, c: (token_partner(x, c), c))
    cross = moved(own, lambda x, c: (token_partner(x, 1 - c), 1 - c))
    sib = to_sibling(own)
    return own, sib, same, cross


def reduce_rows(p_own, p_sib, p_same, p_cross):
    same = moved(p_same, lambda x, c: (token_partner(x, c), c))
    cross = moved(p_cross, lambda x, c: (token_partner(x, c), 1 - c))
    sib = to_sibling(p_sib)
    total = p_own.astype(jnp.float32) + sib.astype(jnp.float32)
    total = total + same.astype(jnp.float32) + cross.astype(jnp.float32)
    return total.astype(jnp.bfloat16)


def on_device(
    pre_gate_a, pre_gate_b, pre_up_a, pre_up_b, grads_a, grads_b,
    route_a, route_b, probs_a, probs_b, w_gate, w_up, w_down,
):
    upper = passed_along(grads_a[0], -1)
    lower = passed_along(grads_b[0], 1)
    me = lax.axis_index("expert")
    core = me % NC
    x = (me // NC) % NX
    mate = weight_partner(x, core)
    pos = jnp.stack([x, core, token_partner(x, core)]).astype(jnp.int32)
    pre = [v[0].reshape(-1, CAP, v.shape[-1]) for v in (pre_gate_a, pre_up_a, pre_gate_b, pre_up_b)]

    def wanted(v):
        grid = v.reshape(EXPERTS, NX, NC, CAP, v.shape[-1])
        pair = [lax.dynamic_index_in_dim(grid, k, 1, False) for k in (mate, (x + 2) % NX)]
        return jnp.stack(pair)

    weights = []
    for w in (w_down[0], w_gate[0], w_up[0]):
        weights += [w, to_weight_partner(w)]
    far = to_weight_partner(jnp.stack([wanted(v) for v in pre]))
    far = far.reshape(len(pre), -1, CAP, far.shape[-1])

    def handle(arrived, route, probs, saved):
        chosen = table(slots_of(route))
        send = lax.dot_general(
            chosen, arrived, (((0,), (0,)), ((), ())), preferred_element_type=jnp.float32
        ).astype(jnp.bfloat16)
        wide = send.shape[-1]
        own = over_z(send.reshape(EXPERTS, CAP, wide)).reshape(EXPERTS * CAP, wide)
        pieces = gather_rows(own)
        parts = expert_work(pos, pieces, saved, weights)
        total = reduce_rows(*parts)
        back = over_z(total.reshape(EXPERTS, CAP, -1)).reshape(EXPERTS * CAP, -1)
        picked = jnp.dot(chosen, back, preferred_element_type=jnp.float32)
        grad_x = (probs * picked[:, :wide]).astype(jnp.bfloat16)
        return grad_x[None], picked[None, :, wide:wide + 1]

    dx_a, dprob_a = handle(upper, route_a[0], probs_a[0], (pre[0], pre[1], far[0], far[1]))
    dx_b, dprob_b = handle(lower, route_b[0], probs_b[0], (pre[2], pre[3], far[2], far[3]))
    return (dx_a, dx_b, dprob_a, dprob_b)


def solution(mesh):
    hidden = P("section", None, "expert")
    tokens = P("section", "expert", None)

    return jax.shard_map(
        on_device,
        mesh=mesh,
        in_specs=(hidden,) * 4 + (tokens,) * 6 + (hidden, hidden, tokens),
        out_specs=(tokens,) * 4,
        check_vma=False,
    )
```

```python
import functools

import jax
import jax.numpy as jnp
from jax import lax
from jax.experimental import pallas as pl
from jax.experimental.pallas import tpu as pltpu
from jax.sharding import PartitionSpec as P

EXPERTS = 4
CAP = 16
NX = 4
NC = 2
PAD = 128
TILE = 512


def place(z, x, c):
    return z * NX * NC + x * NC + c


def weight_partner(x, c):
    return (((x + c) ^ 1) + NX - c) % NX


def token_partner(x, c):
    return weight_partner(x, 1 - c)


def moved(value, rule):
    pairs = []
    for z in range(EXPERTS):
        for x in range(NX):
            for c in range(NC):
                to_x, to_c = rule(x, c)
                pairs.append((place(z, x, c), place(z, to_x, to_c)))
    return lax.ppermute(value, "expert", pairs)


def to_weight_partner(value):
    return moved(value, lambda x, c: (weight_partner(x, c), c))


def to_sibling(value):
    return moved(value, lambda x, c: (x, 1 - c))


def over_z(value):
    columns = [[place(z, x, c) for z in range(EXPERTS)] for x in range(NX) for c in range(NC)]
    return lax.all_to_all(
        value, "expert", split_axis=0, concat_axis=0, axis_index_groups=columns, tiled=True
    )


def passed_along(value, steps):
    count = lax.axis_size("section")
    pairs = [(source, (source + steps) % count) for source in range(count)]
    return lax.ppermute(value, "section", pairs)


def slots_of(route):
    onehot = (route == jnp.arange(EXPERTS, dtype=jnp.int32)[None, :]).astype(jnp.float32)
    size = onehot.shape[0]
    before = jnp.tril(jnp.ones((size, size), jnp.float32), -1)
    rank = jnp.dot(before, onehot)
    slot = jnp.sum(rank * onehot, axis=-1, keepdims=True).astype(jnp.int32)
    return route * CAP + slot


def table(place_of):
    lanes = jnp.arange(EXPERTS * CAP, dtype=jnp.int32)[None, :]
    return (place_of == lanes).astype(jnp.bfloat16)


def nt(a, b):
    return lax.dot_general(a, b, (((1,), (1,)), ((), ())), preferred_element_type=jnp.float32)


CUTS = (0, 1024, 2048, 3072, 3584)


def cuts_of(wide):
    return [c for c in CUTS if c < wide] + [wide]


def expert_kernel(
    pos, own, sib, same, cross, gate_own, up_own, far,
    wd_own, wd_mate, wg_own, wg_mate, wu_own, wu_mate,
    p_own, p_sib, p_same, p_cross,
    v_rows, v_near, v_far, v_wd, v_w, v_out, s_in, s_saved, s_w, s_out, *, which,
):
    x, c, tp = pos[0], pos[1], pos[2]
    n, wide = own.shape
    unit = wd_own.shape[0]
    cuts = cuts_of(wide)
    spans = [pl.ds(lo, hi - lo) for lo, hi in zip(cuts, cuts[1:])]
    incoming, later = [], []
    for i, span in enumerate(spans):
        group = []
        for k, ref in enumerate((own, sib, same, cross)):
            group.append((ref.at[:, span], v_rows.at[pl.ds(k * n, n), span]))
        for k, ref in enumerate((wd_own, wd_mate)):
            group.append((ref.at[:, span], v_wd.at[pl.ds(k * unit, unit), span]))
        incoming.append([pltpu.make_async_copy(a, b, s_in.at[i, k]) for k, (a, b) in enumerate(group)])
    keep = [(gate_own, v_near.at[0]), (up_own, v_near.at[1])]
    keep.append((far.at[pl.ds(2 * which, 2)], v_far))
    keep = [pltpu.make_async_copy(a, b, s_saved.at[k]) for k, (a, b) in enumerate(keep)]
    for i, span in enumerate(spans):
        later.append(
            [
                pltpu.make_async_copy(ref.at[span], v_w.at[k, span], s_w.at[i, k])
                for k, ref in enumerate((wg_own, wg_mate, wu_own, wu_mate))
            ]
        )
    for group in incoming + [keep] + later:
        for copy in group:
            copy.start()
    dh = None
    for i, (lo, hi) in enumerate(zip(cuts, cuts[1:])):
        for copy in incoming[i]:
            copy.wait()
        for d in range(lo, hi, TILE):
            cut = slice(d, d + TILE)
            term = nt(v_rows[:, cut], v_wd[:, cut])
            dh = term if dh is None else dh + term
    for copy in keep:
        copy.wait()

    def saved(k):
        blocks = []
        for slot, xs in ((0, x), (1, tp)):
            for cs in (c, 1 - c):
                for z in range(EXPERTS):
                    near = v_near[k, z * NX * NC + xs * NC + cs]
                    away = v_far[k, (slot * EXPERTS + z) * NC + cs]
                    blocks.append(jnp.concatenate([near, away], axis=-1))
        return jnp.concatenate(blocks, axis=0).astype(jnp.float32)

    gate = saved(0)
    up = saved(1)
    sig = jax.nn.sigmoid(gate)
    act = gate * sig
    slope = sig * (1.0 + gate * (1.0 - sig))
    q = jnp.sum(dh * (act * up), axis=-1, keepdims=True)
    dg = (dh * up * slope).astype(jnp.bfloat16)
    du = (dh * act).astype(jnp.bfloat16)
    both = jnp.concatenate([dg, du], axis=-1)
    v_out[:, wide:] = jnp.broadcast_to(q, (q.shape[0], PAD)).astype(jnp.bfloat16)
    stores = []
    for i, (lo, hi) in enumerate(zip(cuts, cuts[1:])):
        for copy in later[i]:
            copy.wait()
        for d in range(lo, hi, TILE):
            cut = slice(d, d + TILE)
            w = jnp.concatenate([v_w[k, cut] for k in range(4)], axis=-1)
            v_out[:, cut] = nt(both, w).astype(jnp.bfloat16)
        size = hi - lo + (PAD if hi == wide else 0)
        for k, out in enumerate((p_same, p_cross, p_sib, p_own)):
            row = (2, 3, 1, 0)[k] * n
            copy = pltpu.make_async_copy(
                v_out.at[pl.ds(row, n), pl.ds(lo, size)], out.at[:, pl.ds(lo, size)], s_out.at[i, k]
            )
            copy.start()
            stores.append(copy)
    for copy in stores:
        copy.wait()


def expert_work(pos, pieces, near, far, weights, which):
    count, wide = pieces[0].shape
    unit = weights[0].shape[0]
    shape = jax.ShapeDtypeStruct((count, wide + PAD), jnp.bfloat16)
    anywhere = pl.BlockSpec(memory_space=pl.ANY)
    bf16 = jnp.bfloat16
    steps = len(cuts_of(wide)) - 1
    return pl.pallas_call(
        functools.partial(expert_kernel, which=which),
        in_specs=[pl.BlockSpec(memory_space=pltpu.SMEM)] + [anywhere] * 13,
        out_specs=[anywhere] * 4,
        out_shape=[shape] * 4,
        scratch_shapes=[
            pltpu.VMEM((4 * count, wide), bf16),
            pltpu.VMEM((2,) + near[0].shape, bf16),
            pltpu.VMEM((2,) + far.shape[1:], bf16),
            pltpu.VMEM((2 * unit, wide), bf16),
            pltpu.VMEM((4, wide, unit), bf16),
            pltpu.VMEM((4 * count, wide + PAD), bf16),
            pltpu.SemaphoreType.DMA((steps, 6)),
            pltpu.SemaphoreType.DMA((3,)),
            pltpu.SemaphoreType.DMA((steps, 4)),
            pltpu.SemaphoreType.DMA((steps, 4)),
        ],
        compiler_params=pltpu.CompilerParams(vmem_limit_bytes=32 << 20),
        name="expert_work",
    )(pos, *pieces, *near, far, *weights)


def unpack_kernel(chosen, back, probs, grad_x, grad_p):
    wide = grad_x.shape[-1]
    picked = jnp.dot(chosen[...], back[:, :wide], preferred_element_type=jnp.float32)
    grad_x[...] = (probs[...] * picked).astype(jnp.bfloat16)
    shares = back[:, wide:].astype(jnp.float32).T.astype(jnp.bfloat16)
    grad_p[...] = nt(shares, chosen[...])[:1]


def unpack(chosen, back, probs):
    count = chosen.shape[0]
    vmem = pl.BlockSpec(memory_space=pltpu.VMEM)
    return pl.pallas_call(
        unpack_kernel,
        in_specs=[vmem] * 3,
        out_specs=[vmem] * 2,
        out_shape=[
            jax.ShapeDtypeStruct((count, back.shape[-1] - PAD), jnp.bfloat16),
            jax.ShapeDtypeStruct((1, count), jnp.float32),
        ],
        compiler_params=pltpu.CompilerParams(vmem_limit_bytes=8 << 20),
        name="unpack",
    )(chosen, back, probs)


def gather_rows(own):
    same = moved(own, lambda x, c: (token_partner(x, c), c))
    cross = moved(own, lambda x, c: (token_partner(x, 1 - c), 1 - c))
    sib = to_sibling(own)
    return own, sib, same, cross


def reduce_rows(p_own, p_sib, p_same, p_cross):
    same = moved(p_same, lambda x, c: (token_partner(x, c), c))
    cross = moved(p_cross, lambda x, c: (token_partner(x, c), 1 - c))
    sib = to_sibling(p_sib)
    total = p_own.astype(jnp.float32) + sib.astype(jnp.float32)
    total = total + same.astype(jnp.float32) + cross.astype(jnp.float32)
    return total.astype(jnp.bfloat16)


def on_device(
    pre_gate_a, pre_gate_b, pre_up_a, pre_up_b, grads_a, grads_b,
    route_a, route_b, probs_a, probs_b, w_gate, w_up, w_down,
):
    upper = passed_along(grads_a[0], -1)
    lower = passed_along(grads_b[0], 1)
    me = lax.axis_index("expert")
    core = me % NC
    x = (me // NC) % NX
    mate = weight_partner(x, core)
    pos = jnp.stack([x, core, token_partner(x, core)]).astype(jnp.int32)
    pre = [v[0].reshape(-1, CAP, v.shape[-1]) for v in (pre_gate_a, pre_up_a, pre_gate_b, pre_up_b)]

    def wanted(v):
        grid = v.reshape(EXPERTS, NX, NC, CAP, v.shape[-1])
        pair = [lax.dynamic_index_in_dim(grid, k, 1, False) for k in (mate, (x + 2) % NX)]
        return jnp.stack(pair)

    weights = []
    for w in (w_down[0], w_gate[0], w_up[0]):
        weights += [w, to_weight_partner(w)]
    far = to_weight_partner(jnp.stack([wanted(v) for v in pre]))
    far = far.reshape(len(pre), -1, CAP, far.shape[-1])

    def handle(arrived, route, probs, near, which):
        chosen = table(slots_of(route))
        send = lax.dot_general(
            chosen, arrived, (((0,), (0,)), ((), ())), preferred_element_type=jnp.float32
        ).astype(jnp.bfloat16)
        wide = send.shape[-1]
        own = over_z(send.reshape(EXPERTS, CAP, wide)).reshape(EXPERTS * CAP, wide)
        pieces = gather_rows(own)
        parts = expert_work(pos, pieces, near, far, weights, which)
        total = reduce_rows(*parts)
        back = over_z(total.reshape(EXPERTS, CAP, -1)).reshape(EXPERTS * CAP, -1)
        grad_x, grad_p = unpack(chosen, back, probs)
        return grad_x[None], grad_p[..., None]

    dx_a, dprob_a = handle(upper, route_a[0], probs_a[0], (pre[0], pre[1]), 0)
    dx_b, dprob_b = handle(lower, route_b[0], probs_b[0], (pre[2], pre[3]), 1)
    return (dx_a, dx_b, dprob_a, dprob_b)


def solution(mesh):
    hidden = P("section", None, "expert")
    tokens = P("section", "expert", None)

    return jax.shard_map(
        on_device,
        mesh=mesh,
        in_specs=(hidden,) * 4 + (tokens,) * 6 + (hidden, hidden, tokens),
        out_specs=(tokens,) * 4,
        check_vma=False,
    )
```

```python
import functools

import jax
import jax.numpy as jnp
from jax import lax
from jax.experimental import pallas as pl
from jax.experimental.pallas import tpu as pltpu
from jax.sharding import PartitionSpec as P

EXPERTS = 4
CAP = 16
NX = 4
NC = 2
PAD = 128
TILE = 512


def place(z, x, c):
    return z * NX * NC + x * NC + c


def weight_partner(x, c):
    return (((x + c) ^ 1) + NX - c) % NX


def token_partner(x, c):
    return weight_partner(x, 1 - c)


def moved(value, rule):
    pairs = []
    for z in range(EXPERTS):
        for x in range(NX):
            for c in range(NC):
                to_x, to_c = rule(x, c)
                pairs.append((place(z, x, c), place(z, to_x, to_c)))
    return lax.ppermute(value, "expert", pairs)


def to_weight_partner(value):
    return moved(value, lambda x, c: (weight_partner(x, c), c))


def to_sibling(value):
    return moved(value, lambda x, c: (x, 1 - c))


def over_z(value):
    columns = [[place(z, x, c) for z in range(EXPERTS)] for x in range(NX) for c in range(NC)]
    return lax.all_to_all(
        value, "expert", split_axis=0, concat_axis=0, axis_index_groups=columns, tiled=True
    )


def along_z(value, dz):
    return lax.ppermute(
        value,
        "expert",
        [
            (place(z, x, c), place((z + dz) % EXPERTS, x, c))
            for z in range(EXPERTS)
            for x in range(NX)
            for c in range(NC)
        ],
    )


def exchange_z(blocks):
    arrived = [blocks[0]]
    for dz in range(1, EXPERTS):
        arrived.append(along_z(blocks[dz], dz))
    return arrived


def passed_along(value, steps):
    count = lax.axis_size("section")
    pairs = [(source, (source + steps) % count) for source in range(count)]
    return lax.ppermute(value, "section", pairs)


def slots_of(route):
    onehot = (route == jnp.arange(EXPERTS, dtype=jnp.int32)[None, :]).astype(jnp.float32)
    size = onehot.shape[0]
    before = jnp.tril(jnp.ones((size, size), jnp.float32), -1)
    rank = jnp.dot(before, onehot)
    slot = jnp.sum(rank * onehot, axis=-1, keepdims=True).astype(jnp.int32)
    return route * CAP + slot


def table(place_of):
    lanes = jnp.arange(EXPERTS * CAP, dtype=jnp.int32)[None, :]
    return (place_of == lanes).astype(jnp.bfloat16)


def nt(a, b):
    return lax.dot_general(a, b, (((1,), (1,)), ((), ())), preferred_element_type=jnp.float32)


def expert_kernel(
    pos, own, sib, same, cross, gate_own, up_own, far,
    wd_own, wd_mate, wg_own, wg_mate, wu_own, wu_mate,
    p_own, p_sib, p_same, p_cross, *, which,
):
    x, c, tp = pos[0], pos[1], pos[2]
    n, wide = own.shape
    dh = None
    for d in range(0, wide, TILE):
        cut = slice(d, d + TILE)
        rows = jnp.concatenate([own[:, cut], sib[:, cut], same[:, cut], cross[:, cut]], axis=0)
        wd = jnp.concatenate([wd_own[:, cut], wd_mate[:, cut]], axis=0)
        term = nt(rows, wd)
        dh = term if dh is None else dh + term

    def saved(near, k):
        blocks = []
        for slot, xs in ((0, x), (1, tp)):
            for cs in (c, 1 - c):
                for z in range(EXPERTS):
                    mine = near[z * NX * NC + xs * NC + cs]
                    away = far[2 * which + k, (slot * EXPERTS + z) * NC + cs]
                    blocks.append(jnp.concatenate([mine, away], axis=-1))
        return jnp.concatenate(blocks, axis=0).astype(jnp.float32)

    gate = saved(gate_own, 0)
    up = saved(up_own, 1)
    sig = jax.nn.sigmoid(gate)
    act = gate * sig
    slope = sig * (1.0 + gate * (1.0 - sig))
    q = jnp.sum(dh * (act * up), axis=-1, keepdims=True)
    dg = (dh * up * slope).astype(jnp.bfloat16)
    du = (dh * act).astype(jnp.bfloat16)
    both = jnp.concatenate([dg, du], axis=-1)
    outs = (p_own, p_sib, p_same, p_cross)
    for d in range(0, wide, TILE):
        cut = slice(d, d + TILE)
        w = jnp.concatenate([wg_own[cut], wg_mate[cut], wu_own[cut], wu_mate[cut]], axis=-1)
        part = nt(both, w).astype(jnp.bfloat16)
        for k, out in enumerate(outs):
            out[:, cut] = part[k * n:(k + 1) * n]
    q = jnp.broadcast_to(q, (q.shape[0], PAD)).astype(jnp.bfloat16)
    for k, out in enumerate(outs):
        out[:, wide:] = q[k * n:(k + 1) * n]


def expert_work(pos, pieces, near, far, weights, which):
    count, wide = pieces[0].shape
    shape = jax.ShapeDtypeStruct((count, wide + PAD), jnp.bfloat16)
    vmem = pl.BlockSpec(memory_space=pltpu.VMEM)
    return pl.pallas_call(
        functools.partial(expert_kernel, which=which),
        in_specs=[pl.BlockSpec(memory_space=pltpu.SMEM)] + [vmem] * 13,
        out_specs=[vmem] * 4,
        out_shape=[shape] * 4,
        compiler_params=pltpu.CompilerParams(vmem_limit_bytes=20 << 20),
        name="expert_work",
    )(pos, *pieces, *near, far, *weights)


def total_kernel(pos, own, sib, same, cross, *outs):
    for k, out in enumerate(outs):
        z = pos[k]
        total = own[z].astype(jnp.float32) + sib[z].astype(jnp.float32)
        total = total + same[z].astype(jnp.float32) + cross[z].astype(jnp.float32)
        out[...] = total.astype(jnp.bfloat16)


def total_blocks(pos, parts):
    wide = parts[0].shape[1]
    parts = [v.reshape(EXPERTS, CAP, wide) for v in parts]
    vmem = pl.BlockSpec(memory_space=pltpu.VMEM)
    return pl.pallas_call(
        total_kernel,
        in_specs=[pl.BlockSpec(memory_space=pltpu.SMEM)] + [vmem] * 4,
        out_specs=[vmem] * EXPERTS,
        out_shape=[jax.ShapeDtypeStruct((CAP, wide), jnp.bfloat16)] * EXPERTS,
        compiler_params=pltpu.CompilerParams(vmem_limit_bytes=8 << 20),
        name="total_blocks",
    )(pos, *parts)


def unpack_kernel(chosen, probs, *refs):
    grad_x, grad_p = refs[-2:]
    wide = grad_x.shape[-1]
    back = jnp.concatenate([ref[...] for ref in refs[:-2]], axis=0)
    picked = jnp.dot(chosen[...], back[:, :wide], preferred_element_type=jnp.float32)
    grad_x[...] = (probs[...] * picked).astype(jnp.bfloat16)
    shares = back[:, wide:].astype(jnp.float32).T.astype(jnp.bfloat16)
    grad_p[...] = nt(shares, chosen[...])[:1]


def unpack(chosen, probs, *blocks):
    count = chosen.shape[0]
    vmem = pl.BlockSpec(memory_space=pltpu.VMEM)
    grad_x, grad_p = pl.pallas_call(
        unpack_kernel,
        in_specs=[vmem] * (2 + len(blocks)),
        out_specs=[vmem] * 2,
        out_shape=[
            jax.ShapeDtypeStruct((count, blocks[0].shape[-1] - PAD), jnp.bfloat16),
            jax.ShapeDtypeStruct((1, count), jnp.float32),
        ],
        compiler_params=pltpu.CompilerParams(vmem_limit_bytes=8 << 20),
        name="unpack",
    )(chosen, probs, *blocks)
    return grad_x[None], grad_p[..., None]


def gather_rows(own):
    same = moved(own, lambda x, c: (token_partner(x, c), c))
    cross = moved(own, lambda x, c: (token_partner(x, 1 - c), 1 - c))
    sib = to_sibling(own)
    return own, sib, same, cross


def reduce_rows(p_own, p_sib, p_same, p_cross):
    same = moved(p_same, lambda x, c: (token_partner(x, c), c))
    cross = moved(p_cross, lambda x, c: (token_partner(x, c), 1 - c))
    sib = to_sibling(p_sib)
    return p_own, sib, same, cross


def total_of(parts):
    total = parts[0].astype(jnp.float32) + parts[1].astype(jnp.float32)
    total = total + parts[2].astype(jnp.float32) + parts[3].astype(jnp.float32)
    return total.astype(jnp.bfloat16)


def on_device(
    pre_gate_a, pre_gate_b, pre_up_a, pre_up_b, grads_a, grads_b,
    route_a, route_b, probs_a, probs_b, w_gate, w_up, w_down,
):
    upper = passed_along(grads_a, -1)
    lower = passed_along(grads_b, 1)
    me = lax.axis_index("expert")
    core = me % NC
    x = (me // NC) % NX
    mate = weight_partner(x, core)
    pos = jnp.stack([x, core, token_partner(x, core)]).astype(jnp.int32)
    pre = [v[0].reshape(-1, CAP, v.shape[-1]) for v in (pre_gate_a, pre_up_a, pre_gate_b, pre_up_b)]

    def wanted(v):
        grid = v.reshape(EXPERTS, NX, NC, CAP, v.shape[-1])
        pair = [lax.dynamic_index_in_dim(grid, k, 1, False) for k in (mate, (x + 2) % NX)]
        return jnp.stack(pair)

    weights = []
    for w in (w_down[0], w_gate[0], w_up[0]):
        weights += [w, to_weight_partner(w)]
    far = to_weight_partner(jnp.stack([wanted(v) for v in pre]))
    far = far.reshape(len(pre), -1, CAP, far.shape[-1])

    home = me // (NX * NC)
    order = jnp.arange(EXPERTS, dtype=jnp.int32)
    ahead = ((home + order) % EXPERTS).astype(jnp.int32)
    wide = upper.shape[-1]

    def partials(own, near, which):
        pieces = gather_rows(own)
        parts = expert_work(pos, pieces, near, far, weights, which)
        return reduce_rows(*parts)

    chosen_a = table(slots_of(route_a[0]))
    send_a = lax.dot_general(
        chosen_a, upper[0], (((0,), (0,)), ((), ())), preferred_element_type=jnp.float32
    ).astype(jnp.bfloat16)
    own_a = over_z(send_a.reshape(EXPERTS, CAP, wide)).reshape(EXPERTS * CAP, wide)
    total_a = total_of(partials(own_a, (pre[0], pre[1]), 0))
    back_a = over_z(total_a.reshape(EXPERTS, CAP, -1)).reshape(EXPERTS * CAP, -1)
    dx_a, dprob_a = unpack(chosen_a, probs_a[0], back_a)

    slot_b = slots_of(route_b[0])
    send_b = lax.dot_general(
        table(slot_b), lower[0], (((0,), (0,)), ((), ())), preferred_element_type=jnp.float32
    ).astype(jnp.bfloat16)
    own_b = over_z(send_b.reshape(EXPERTS, CAP, wide)).reshape(EXPERTS * CAP, wide)
    parts_b = partials(own_b, (pre[2], pre[3]), 1)
    back_b = exchange_z(total_blocks(ahead, parts_b))
    turned = (home - slot_b // CAP) % EXPERTS * CAP + slot_b % CAP
    dx_b, dprob_b = unpack(table(turned), probs_b[0], *back_b)
    return (dx_a, dx_b, dprob_a, dprob_b)


def solution(mesh):
    hidden = P("section", None, "expert")
    tokens = P("section", "expert", None)

    return jax.shard_map(
        on_device,
        mesh=mesh,
        in_specs=(hidden,) * 4 + (tokens,) * 6 + (hidden, hidden, tokens),
        out_specs=(tokens,) * 4,
        check_vma=False,
    )
```

```python
import functools

import jax
import jax.numpy as jnp
from jax import lax
from jax.experimental import pallas as pl
from jax.experimental.pallas import tpu as pltpu
from jax.sharding import PartitionSpec as P

EXPERTS = 4
CAP = 16
NX = 4
NC = 2
PAD = 128
TILE = 512


def place(z, x, c):
    return z * NX * NC + x * NC + c


def weight_partner(x, c):
    return (((x + c) ^ 1) + NX - c) % NX


def token_partner(x, c):
    return weight_partner(x, 1 - c)


def moved(value, rule):
    pairs = []
    for z in range(EXPERTS):
        for x in range(NX):
            for c in range(NC):
                to_x, to_c = rule(x, c)
                pairs.append((place(z, x, c), place(z, to_x, to_c)))
    return lax.ppermute(value, "expert", pairs)


def to_weight_partner(value):
    return moved(value, lambda x, c: (weight_partner(x, c), c))


def to_sibling(value):
    return moved(value, lambda x, c: (x, 1 - c))


def over_z(value):
    columns = [[place(z, x, c) for z in range(EXPERTS)] for x in range(NX) for c in range(NC)]
    return lax.all_to_all(
        value, "expert", split_axis=0, concat_axis=0, axis_index_groups=columns, tiled=True
    )


def along_z(value, dz):
    return lax.ppermute(
        value,
        "expert",
        [
            (place(z, x, c), place((z + dz) % EXPERTS, x, c))
            for z in range(EXPERTS)
            for x in range(NX)
            for c in range(NC)
        ],
    )


def exchange_z(blocks):
    arrived = [blocks[0]]
    for dz in range(1, EXPERTS):
        arrived.append(along_z(blocks[dz], dz))
    return arrived


def passed_along(value, steps):
    count = lax.axis_size("section")
    pairs = [(source, (source + steps) % count) for source in range(count)]
    return lax.ppermute(value, "section", pairs)


def slots_of(route):
    onehot = (route == jnp.arange(EXPERTS, dtype=jnp.int32)[None, :]).astype(jnp.float32)
    size = onehot.shape[0]
    before = jnp.tril(jnp.ones((size, size), jnp.float32), -1)
    rank = jnp.dot(before, onehot)
    slot = jnp.sum(rank * onehot, axis=-1, keepdims=True).astype(jnp.int32)
    return route * CAP + slot


def table(place_of):
    lanes = jnp.arange(EXPERTS * CAP, dtype=jnp.int32)[None, :]
    return (place_of == lanes).astype(jnp.bfloat16)


def nt(a, b):
    return lax.dot_general(a, b, (((1,), (1,)), ((), ())), preferred_element_type=jnp.float32)


def expert_kernel(
    pos, near_all, far_all, own, sib, same, cross,
    wd_own, wd_mate, wg_own, wg_mate, wu_own, wu_mate,
    p_own, p_sib, p_same, p_cross, near, far, arrived, *, which,
):
    x, c, tp = pos[0], pos[1], pos[2]
    n, wide = own.shape
    loads = [
        pltpu.make_async_copy(ref.at[pl.ds(2 * which, 2)], buf, arrived.at[k])
        for k, (ref, buf) in enumerate(((near_all, near), (far_all, far)))
    ]
    for load in loads:
        load.start()
    dh = None
    for d in range(0, wide, TILE):
        cut = slice(d, d + TILE)
        rows = jnp.concatenate([own[:, cut], sib[:, cut], same[:, cut], cross[:, cut]], axis=0)
        wd = jnp.concatenate([wd_own[:, cut], wd_mate[:, cut]], axis=0)
        term = nt(rows, wd)
        dh = term if dh is None else dh + term

    for load in loads:
        load.wait()

    def saved(k):
        blocks = []
        for slot, xs in ((0, x), (1, tp)):
            for cs in (c, 1 - c):
                for z in range(EXPERTS):
                    mine = near[k, z * NX * NC + xs * NC + cs]
                    away = far[k, (slot * EXPERTS + z) * NC + cs]
                    blocks.append(jnp.concatenate([mine, away], axis=-1))
        return jnp.concatenate(blocks, axis=0).astype(jnp.float32)

    gate = saved(0)
    up = saved(1)
    sig = jax.nn.sigmoid(gate)
    act = gate * sig
    slope = sig * (1.0 + gate * (1.0 - sig))
    q = jnp.sum(dh * (act * up), axis=-1, keepdims=True)
    dg = (dh * up * slope).astype(jnp.bfloat16)
    du = (dh * act).astype(jnp.bfloat16)
    both = jnp.concatenate([dg, du], axis=-1)
    outs = (p_own, p_sib, p_same, p_cross)
    for d in range(0, wide, TILE):
        cut = slice(d, d + TILE)
        w = jnp.concatenate([wg_own[cut], wg_mate[cut], wu_own[cut], wu_mate[cut]], axis=-1)
        part = nt(both, w).astype(jnp.bfloat16)
        for k, out in enumerate(outs):
            out[:, cut] = part[k * n:(k + 1) * n]
    q = jnp.broadcast_to(q, (q.shape[0], PAD)).astype(jnp.bfloat16)
    for k, out in enumerate(outs):
        out[:, wide:] = q[k * n:(k + 1) * n]


def expert_work(pos, pieces, near, far, weights, which):
    count, wide = pieces[0].shape
    shape = jax.ShapeDtypeStruct((count, wide + PAD), jnp.bfloat16)
    vmem = pl.BlockSpec(memory_space=pltpu.VMEM)
    return pl.pallas_call(
        functools.partial(expert_kernel, which=which),
        in_specs=[pl.BlockSpec(memory_space=pltpu.SMEM)]
        + [pl.BlockSpec(memory_space=pl.ANY)] * 2
        + [vmem] * 10,
        out_specs=[vmem] * 4,
        out_shape=[shape] * 4,
        scratch_shapes=[
            pltpu.VMEM((2,) + near.shape[1:], near.dtype),
            pltpu.VMEM((2,) + far.shape[1:], far.dtype),
            pltpu.SemaphoreType.DMA((2,)),
        ],
        compiler_params=pltpu.CompilerParams(vmem_limit_bytes=20 << 20),
        name="expert_work",
    )(pos, near, far, *pieces, *weights)


def total_kernel(pos, own, sib, same, cross, *outs):
    for k, out in enumerate(outs):
        z = pos[k]
        total = own[z].astype(jnp.float32) + sib[z].astype(jnp.float32)
        total = total + same[z].astype(jnp.float32) + cross[z].astype(jnp.float32)
        out[...] = total.astype(jnp.bfloat16)


def total_blocks(pos, parts):
    wide = parts[0].shape[1]
    parts = [v.reshape(EXPERTS, CAP, wide) for v in parts]
    vmem = pl.BlockSpec(memory_space=pltpu.VMEM)
    return pl.pallas_call(
        total_kernel,
        in_specs=[pl.BlockSpec(memory_space=pltpu.SMEM)] + [vmem] * 4,
        out_specs=[vmem] * EXPERTS,
        out_shape=[jax.ShapeDtypeStruct((CAP, wide), jnp.bfloat16)] * EXPERTS,
        compiler_params=pltpu.CompilerParams(vmem_limit_bytes=8 << 20),
        name="total_blocks",
    )(pos, *parts)


def unpack_kernel(chosen, probs, *refs):
    grad_x, grad_p = refs[-2:]
    wide = grad_x.shape[-1]
    back = jnp.concatenate([ref[...] for ref in refs[:-2]], axis=0)
    picked = jnp.dot(chosen[...], back[:, :wide], preferred_element_type=jnp.float32)
    grad_x[...] = (probs[...] * picked).astype(jnp.bfloat16)
    shares = back[:, wide:].astype(jnp.float32).T.astype(jnp.bfloat16)
    grad_p[...] = nt(shares, chosen[...])[:1]


def unpack(chosen, probs, *blocks):
    count = chosen.shape[0]
    vmem = pl.BlockSpec(memory_space=pltpu.VMEM)
    grad_x, grad_p = pl.pallas_call(
        unpack_kernel,
        in_specs=[vmem] * (2 + len(blocks)),
        out_specs=[vmem] * 2,
        out_shape=[
            jax.ShapeDtypeStruct((count, blocks[0].shape[-1] - PAD), jnp.bfloat16),
            jax.ShapeDtypeStruct((1, count), jnp.float32),
        ],
        compiler_params=pltpu.CompilerParams(vmem_limit_bytes=8 << 20),
        name="unpack",
    )(chosen, probs, *blocks)
    return grad_x[None], grad_p[..., None]


def gather_rows(own):
    same = moved(own, lambda x, c: (token_partner(x, c), c))
    cross = moved(own, lambda x, c: (token_partner(x, 1 - c), 1 - c))
    sib = to_sibling(own)
    return own, sib, same, cross


def reduce_rows(p_own, p_sib, p_same, p_cross):
    same = moved(p_same, lambda x, c: (token_partner(x, c), c))
    cross = moved(p_cross, lambda x, c: (token_partner(x, c), 1 - c))
    sib = to_sibling(p_sib)
    return p_own, sib, same, cross


def total_of(parts):
    total = parts[0].astype(jnp.float32) + parts[1].astype(jnp.float32)
    total = total + parts[2].astype(jnp.float32) + parts[3].astype(jnp.float32)
    return total.astype(jnp.bfloat16)


def on_device(
    pre_gate_a, pre_gate_b, pre_up_a, pre_up_b, grads_a, grads_b,
    route_a, route_b, probs_a, probs_b, w_gate, w_up, w_down,
):
    upper = passed_along(grads_a, -1)
    lower = passed_along(grads_b, 1)
    me = lax.axis_index("expert")
    core = me % NC
    x = (me // NC) % NX
    mate = weight_partner(x, core)
    pos = jnp.stack([x, core, token_partner(x, core)]).astype(jnp.int32)
    pre = [v[0].reshape(-1, CAP, v.shape[-1]) for v in (pre_gate_a, pre_up_a, pre_gate_b, pre_up_b)]

    def wanted(v):
        grid = v.reshape(EXPERTS, NX, NC, CAP, v.shape[-1])
        pair = [lax.dynamic_index_in_dim(grid, k, 1, False) for k in (mate, (x + 2) % NX)]
        return jnp.stack(pair)

    weights = []
    for w in (w_down[0], w_gate[0], w_up[0]):
        weights += [w, to_weight_partner(w)]
    far = to_weight_partner(jnp.stack([wanted(v) for v in pre]))
    far = far.reshape(len(pre), -1, CAP, far.shape[-1])

    home = me // (NX * NC)
    order = jnp.arange(EXPERTS, dtype=jnp.int32)
    ahead = ((home + order) % EXPERTS).astype(jnp.int32)
    wide = upper.shape[-1]

    near = jnp.stack(pre)

    def partials(own, which):
        pieces = gather_rows(own)
        parts = expert_work(pos, pieces, near, far, weights, which)
        return reduce_rows(*parts)

    chosen_a = table(slots_of(route_a[0]))
    send_a = lax.dot_general(
        chosen_a, upper[0], (((0,), (0,)), ((), ())), preferred_element_type=jnp.float32
    ).astype(jnp.bfloat16)
    own_a = over_z(send_a.reshape(EXPERTS, CAP, wide)).reshape(EXPERTS * CAP, wide)
    total_a = total_of(partials(own_a, 0))
    back_a = over_z(total_a.reshape(EXPERTS, CAP, -1)).reshape(EXPERTS * CAP, -1)
    dx_a, dprob_a = unpack(chosen_a, probs_a[0], back_a)

    slot_b = slots_of(route_b[0])
    send_b = lax.dot_general(
        table(slot_b), lower[0], (((0,), (0,)), ((), ())), preferred_element_type=jnp.float32
    ).astype(jnp.bfloat16)
    own_b = over_z(send_b.reshape(EXPERTS, CAP, wide)).reshape(EXPERTS * CAP, wide)
    parts_b = partials(own_b, 1)
    back_b = exchange_z(total_blocks(ahead, parts_b))
    turned = (home - slot_b // CAP) % EXPERTS * CAP + slot_b % CAP
    dx_b, dprob_b = unpack(table(turned), probs_b[0], *back_b)
    return (dx_a, dx_b, dprob_a, dprob_b)


def solution(mesh):
    hidden = P("section", None, "expert")
    tokens = P("section", "expert", None)

    return jax.shard_map(
        on_device,
        mesh=mesh,
        in_specs=(hidden,) * 4 + (tokens,) * 6 + (hidden, hidden, tokens),
        out_specs=(tokens,) * 4,
        check_vma=False,
    )
```

```python
import functools

import jax
import jax.numpy as jnp
from jax import lax
from jax.experimental import pallas as pl
from jax.experimental.pallas import tpu as pltpu
from jax.sharding import PartitionSpec as P

EXPERTS = 4
CAP = 16
NX = 4
NC = 2
PAD = 128
TILE = 512


def place(z, x, c):
    return z * NX * NC + x * NC + c


def weight_partner(x, c):
    return (((x + c) ^ 1) + NX - c) % NX


def token_partner(x, c):
    return weight_partner(x, 1 - c)


def moved(value, rule):
    pairs = []
    for z in range(EXPERTS):
        for x in range(NX):
            for c in range(NC):
                to_x, to_c = rule(x, c)
                pairs.append((place(z, x, c), place(z, to_x, to_c)))
    return lax.ppermute(value, "expert", pairs)


def to_weight_partner(value):
    return moved(value, lambda x, c: (weight_partner(x, c), c))


def to_sibling(value):
    return moved(value, lambda x, c: (x, 1 - c))


def over_z(value):
    columns = [[place(z, x, c) for z in range(EXPERTS)] for x in range(NX) for c in range(NC)]
    return lax.all_to_all(
        value, "expert", split_axis=0, concat_axis=0, axis_index_groups=columns, tiled=True
    )


def along_z(value, dz):
    return lax.ppermute(
        value,
        "expert",
        [
            (place(z, x, c), place((z + dz) % EXPERTS, x, c))
            for z in range(EXPERTS)
            for x in range(NX)
            for c in range(NC)
        ],
    )


def exchange_z(blocks):
    arrived = [blocks[0]]
    for dz in range(1, EXPERTS):
        arrived.append(along_z(blocks[dz], dz))
    return arrived


def passed_along(value, steps):
    count = lax.axis_size("section")
    pairs = [(source, (source + steps) % count) for source in range(count)]
    return lax.ppermute(value, "section", pairs)


def slots_of(route):
    onehot = (route == jnp.arange(EXPERTS, dtype=jnp.int32)[None, :]).astype(jnp.float32)
    size = onehot.shape[0]
    before = jnp.tril(jnp.ones((size, size), jnp.float32), -1)
    rank = jnp.dot(before, onehot)
    slot = jnp.sum(rank * onehot, axis=-1, keepdims=True).astype(jnp.int32)
    return route * CAP + slot


def table(place_of):
    lanes = jnp.arange(EXPERTS * CAP, dtype=jnp.int32)[None, :]
    return (place_of == lanes).astype(jnp.bfloat16)


def nt(a, b):
    return lax.dot_general(a, b, (((1,), (1,)), ((), ())), preferred_element_type=jnp.float32)


def expert_kernel(
    pos, near_all, far_all, wg_away, wu_away, own, sib, same, cross,
    wd_own, wd_mate, wg_own, wu_own,
    p_own, p_sib, p_same, p_cross, near, far, wg_mate, wu_mate, arrived, *, which,
):
    x, c, tp = pos[0], pos[1], pos[2]
    n, wide = own.shape
    loads = [
        pltpu.make_async_copy(ref.at[pl.ds(2 * which, 2)], buf, arrived.at[k])
        for k, (ref, buf) in enumerate(((near_all, near), (far_all, far)))
    ]
    later = [
        pltpu.make_async_copy(wg_away, wg_mate, arrived.at[2]),
        pltpu.make_async_copy(wu_away, wu_mate, arrived.at[3]),
    ]
    for load in loads + later:
        load.start()
    dh = None
    for d in range(0, wide, TILE):
        cut = slice(d, d + TILE)
        rows = jnp.concatenate([own[:, cut], sib[:, cut], same[:, cut], cross[:, cut]], axis=0)
        wd = jnp.concatenate([wd_own[:, cut], wd_mate[:, cut]], axis=0)
        term = nt(rows, wd)
        dh = term if dh is None else dh + term

    for load in loads:
        load.wait()

    def saved(k):
        blocks = []
        for slot, xs in ((0, x), (1, tp)):
            for cs in (c, 1 - c):
                for z in range(EXPERTS):
                    mine = near[k, z * NX * NC + xs * NC + cs]
                    away = far[k, (slot * EXPERTS + z) * NC + cs]
                    blocks.append(jnp.concatenate([mine, away], axis=-1))
        return jnp.concatenate(blocks, axis=0).astype(jnp.float32)

    gate = saved(0)
    up = saved(1)
    sig = jax.nn.sigmoid(gate)
    act = gate * sig
    slope = sig * (1.0 + gate * (1.0 - sig))
    q = jnp.sum(dh * (act * up), axis=-1, keepdims=True)
    dg = (dh * up * slope).astype(jnp.bfloat16)
    du = (dh * act).astype(jnp.bfloat16)
    both = jnp.concatenate([dg, du], axis=-1)
    for load in later:
        load.wait()
    outs = (p_own, p_sib, p_same, p_cross)
    for d in range(0, wide, TILE):
        cut = slice(d, d + TILE)
        w = jnp.concatenate([wg_own[cut], wg_mate[cut], wu_own[cut], wu_mate[cut]], axis=-1)
        part = nt(both, w).astype(jnp.bfloat16)
        for k, out in enumerate(outs):
            out[:, cut] = part[k * n:(k + 1) * n]
    q = jnp.broadcast_to(q, (q.shape[0], PAD)).astype(jnp.bfloat16)
    for k, out in enumerate(outs):
        out[:, wide:] = q[k * n:(k + 1) * n]


def expert_work(pos, pieces, near, far, weights, which):
    count, wide = pieces[0].shape
    wd, wd_mate, wg, wg_mate, wu, wu_mate = weights
    shape = jax.ShapeDtypeStruct((count, wide + PAD), jnp.bfloat16)
    vmem = pl.BlockSpec(memory_space=pltpu.VMEM)
    return pl.pallas_call(
        functools.partial(expert_kernel, which=which),
        in_specs=[pl.BlockSpec(memory_space=pltpu.SMEM)]
        + [pl.BlockSpec(memory_space=pl.ANY)] * 4
        + [vmem] * 8,
        out_specs=[vmem] * 4,
        out_shape=[shape] * 4,
        scratch_shapes=[
            pltpu.VMEM((2,) + near.shape[1:], near.dtype),
            pltpu.VMEM((2,) + far.shape[1:], far.dtype),
            pltpu.VMEM(wg_mate.shape, wg_mate.dtype),
            pltpu.VMEM(wu_mate.shape, wu_mate.dtype),
            pltpu.SemaphoreType.DMA((4,)),
        ],
        compiler_params=pltpu.CompilerParams(vmem_limit_bytes=20 << 20),
        name="expert_work",
    )(pos, near, far, wg_mate, wu_mate, *pieces, wd, wd_mate, wg, wu)


def total_kernel(pos, own, sib, same, cross, *outs):
    for k, out in enumerate(outs):
        z = pos[k]
        total = own[z].astype(jnp.float32) + sib[z].astype(jnp.float32)
        total = total + same[z].astype(jnp.float32) + cross[z].astype(jnp.float32)
        out[...] = total.astype(jnp.bfloat16)


def total_blocks(pos, parts):
    wide = parts[0].shape[1]
    parts = [v.reshape(EXPERTS, CAP, wide) for v in parts]
    vmem = pl.BlockSpec(memory_space=pltpu.VMEM)
    return pl.pallas_call(
        total_kernel,
        in_specs=[pl.BlockSpec(memory_space=pltpu.SMEM)] + [vmem] * 4,
        out_specs=[vmem] * EXPERTS,
        out_shape=[jax.ShapeDtypeStruct((CAP, wide), jnp.bfloat16)] * EXPERTS,
        compiler_params=pltpu.CompilerParams(vmem_limit_bytes=8 << 20),
        name="total_blocks",
    )(pos, *parts)


def unpack_kernel(chosen, probs, *refs):
    grad_x, grad_p = refs[-2:]
    wide = grad_x.shape[-1]
    back = jnp.concatenate([ref[...] for ref in refs[:-2]], axis=0)
    picked = jnp.dot(chosen[...], back[:, :wide], preferred_element_type=jnp.float32)
    grad_x[...] = (probs[...] * picked).astype(jnp.bfloat16)
    shares = back[:, wide:].astype(jnp.float32).T.astype(jnp.bfloat16)
    grad_p[...] = nt(shares, chosen[...])[:1]


def unpack(chosen, probs, *blocks):
    count = chosen.shape[0]
    vmem = pl.BlockSpec(memory_space=pltpu.VMEM)
    grad_x, grad_p = pl.pallas_call(
        unpack_kernel,
        in_specs=[vmem] * (2 + len(blocks)),
        out_specs=[vmem] * 2,
        out_shape=[
            jax.ShapeDtypeStruct((count, blocks[0].shape[-1] - PAD), jnp.bfloat16),
            jax.ShapeDtypeStruct((1, count), jnp.float32),
        ],
        compiler_params=pltpu.CompilerParams(vmem_limit_bytes=8 << 20),
        name="unpack",
    )(chosen, probs, *blocks)
    return grad_x[None], grad_p[..., None]


def gather_rows(own):
    same = moved(own, lambda x, c: (token_partner(x, c), c))
    cross = moved(own, lambda x, c: (token_partner(x, 1 - c), 1 - c))
    sib = to_sibling(own)
    return own, sib, same, cross


def reduce_rows(p_own, p_sib, p_same, p_cross):
    same = moved(p_same, lambda x, c: (token_partner(x, c), c))
    cross = moved(p_cross, lambda x, c: (token_partner(x, c), 1 - c))
    sib = to_sibling(p_sib)
    return p_own, sib, same, cross


def total_of(parts):
    total = parts[0].astype(jnp.float32) + parts[1].astype(jnp.float32)
    total = total + parts[2].astype(jnp.float32) + parts[3].astype(jnp.float32)
    return total.astype(jnp.bfloat16)


def on_device(
    pre_gate_a, pre_gate_b, pre_up_a, pre_up_b, grads_a, grads_b,
    route_a, route_b, probs_a, probs_b, w_gate, w_up, w_down,
):
    upper = passed_along(grads_a, -1)
    lower = passed_along(grads_b, 1)
    me = lax.axis_index("expert")
    core = me % NC
    x = (me // NC) % NX
    mate = weight_partner(x, core)
    pos = jnp.stack([x, core, token_partner(x, core)]).astype(jnp.int32)
    pre = [v[0].reshape(-1, CAP, v.shape[-1]) for v in (pre_gate_a, pre_up_a, pre_gate_b, pre_up_b)]

    def wanted(v):
        grid = v.reshape(EXPERTS, NX, NC, CAP, v.shape[-1])
        pair = [lax.dynamic_index_in_dim(grid, k, 1, False) for k in (mate, (x + 2) % NX)]
        return jnp.stack(pair)

    weights = []
    for w in (w_down[0], w_gate[0], w_up[0]):
        weights += [w, to_weight_partner(w)]
    far = to_weight_partner(jnp.stack([wanted(v) for v in pre]))
    far = far.reshape(len(pre), -1, CAP, far.shape[-1])

    home = me // (NX * NC)
    order = jnp.arange(EXPERTS, dtype=jnp.int32)
    ahead = ((home + order) % EXPERTS).astype(jnp.int32)
    wide = upper.shape[-1]

    near = jnp.stack(pre)

    def partials(own, which):
        pieces = gather_rows(own)
        parts = expert_work(pos, pieces, near, far, weights, which)
        return reduce_rows(*parts)

    chosen_a = table(slots_of(route_a[0]))
    send_a = lax.dot_general(
        chosen_a, upper[0], (((0,), (0,)), ((), ())), preferred_element_type=jnp.float32
    ).astype(jnp.bfloat16)
    own_a = over_z(send_a.reshape(EXPERTS, CAP, wide)).reshape(EXPERTS * CAP, wide)
    total_a = total_of(partials(own_a, 0))
    back_a = over_z(total_a.reshape(EXPERTS, CAP, -1)).reshape(EXPERTS * CAP, -1)
    dx_a, dprob_a = unpack(chosen_a, probs_a[0], back_a)

    slot_b = slots_of(route_b[0])
    send_b = lax.dot_general(
        table(slot_b), lower[0], (((0,), (0,)), ((), ())), preferred_element_type=jnp.float32
    ).astype(jnp.bfloat16)
    own_b = over_z(send_b.reshape(EXPERTS, CAP, wide)).reshape(EXPERTS * CAP, wide)
    parts_b = partials(own_b, 1)
    back_b = exchange_z(total_blocks(ahead, parts_b))
    turned = (home - slot_b // CAP) % EXPERTS * CAP + slot_b % CAP
    dx_b, dprob_b = unpack(table(turned), probs_b[0], *back_b)
    return (dx_a, dx_b, dprob_a, dprob_b)


def solution(mesh):
    hidden = P("section", None, "expert")
    tokens = P("section", "expert", None)

    return jax.shard_map(
        on_device,
        mesh=mesh,
        in_specs=(hidden,) * 4 + (tokens,) * 6 + (hidden, hidden, tokens),
        out_specs=(tokens,) * 4,
        check_vma=False,
    )
```
